128 devices in a mesh: row: 8 (over y, z_hi), col: 16 (over z_lo, x, core).
Axes of the slice: x: 4, y: 4, z: 4 (z_hi: 2, z_lo: 2; z = z_hi * 2 + z_lo), core: 2. Of those that a mesh axis runs over, the one named last changes fastest.
Arguments:
- known_inverse: float32 [12288, 12288], P('col', 'row'), may hold values from -6 to 6
- factor_sep: float32 [12288, 1536], P('col'), may hold values from -0.09375 to 0.09375
- factor_pair: float32 [1536, 1536], P('col'), may hold values from -0.25 to 0.25
- pivot_inverse: float32 [1536, 1536], P('col', 'row'), may hold values from -6 to 6
- widths: int32 [8], replicated, may hold values from 1 to 512, 1536 in all
- parent_of: int32 [8], replicated, may hold values from -1 to 7, as said below
- ancestors: int32 [8, 24], replicated, may hold values from 0 to 63, all different within a row
Outputs:
- panel_inverse: float32 [1536, 12288], P('col', 'row')
- block_inverse: float32 [1536, 1536], P('col', 'row')
The draws below stay inside these ranges and needn't reach their ends.
Inputs may be any that keep to these rules, and one draw needn't show every extreme that they name: `parent_of`: exactly 4 supernodes have -1; each other one names one of those. `ancestors`: each supernode lists different blocks; every block is listed by some supernode. The widths sum to 1536.
All inputs are finite; a program needn't handle non-finite values.
Results may differ from the reference program's by a relative error of at most 0.0003.
Values sent between devices are 32-bit elements; how exact they have to be, the bound alone decides.
No kernel may reach another device: no remote copies, remote signals or barrier semaphores. Data moves between devices by JAX's collectives and lax.ppermute only.
A program may use at most 128 MiB of HBM per device.

```python
import math
import jax
import jax.numpy as jnp
import numpy as np
from jax import lax

NS = 12288
WTOT = 1536
NSUP = 8
NUP = 4
NBLK = 64
ANC = 24
WMOST = 512


def draw_parent_of(key, part):
    order_key, pick_key = jax.random.split(jax.random.fold_in(key, 11))
    ordering = jax.random.permutation(order_key, NSUP).astype(jnp.int32)
    position = jnp.argsort(ordering).astype(jnp.int32)
    is_upper = position < NUP
    chosen = jax.random.randint(pick_key, (NSUP,), 0, NUP).astype(jnp.int32)
    parents = ordering[chosen]
    return jnp.where(is_upper, -1, parents).astype(jnp.int32)


def steps_of(own_key, extent, cuts, least, top_value):
    def one(dim, parts):
        draws = jax.random.uniform(jax.random.fold_in(jax.random.fold_in(own_key, 6), dim), (parts,), jnp.float32, least / len(cuts), top_value / len(cuts))
        return jnp.repeat(jnp.exp(draws), extent[dim] // parts).reshape((-1,) + (1,) * (len(extent) - dim - 1))

    gain = one(*cuts[0])
    for cut in cuts[1:]:
        gain = gain * one(*cut)
    return gain


def choose_distinct(key, rows, number_of, top, lift):
    ranking = jax.random.permutation(jax.random.fold_in(key, 1), number_of)
    boost = ranking
    for power in range(3):
        boost = boost * boost // number_of
    boost = boost * lift // number_of
    tickets = jax.random.randint(jax.random.fold_in(key, 2), (rows, number_of), 0, 4096) + boost
    holders = jax.random.permutation(jax.random.fold_in(key, 3), rows)[jnp.arange(number_of) % rows]
    tickets = jnp.where(jnp.arange(rows)[:, None] == holders[None, :], 1 << 14, tickets)
    score = tickets * number_of + jnp.arange(number_of)
    return lax.top_k(score.astype(jnp.int32), top)[1].astype(jnp.int32)


def split_up(amount, total, reach, lean):
    loads = [(1 << 20) // math.isqrt(standing ** lean) + 1 for standing in range(2, amount + 1)]
    surplus, holding = total - reach - (amount - 1), [1] * (amount - 1)
    while surplus > 0:
        free = [i for i in range(amount - 1) if holding[i] < reach]
        whole, budget = sum([loads[i] for i in free]), surplus
        for i in free:
            extra = min(reach - holding[i], max(1, budget * loads[i] // whole), surplus)
            holding[i] = holding[i] + extra
            surplus = surplus - extra
    return np.array([reach] + holding)


def uneven_parts(own_key, count, total, most, skew):
    if count == 2:
        one = jax.random.randint(own_key, (), max(1, total - most), min(most, total - 1) + 1)
        return jnp.stack([one, total - one])
    tallies = jnp.asarray(split_up(count, total, most, skew), jnp.int32)
    couples = (count - 1) // 2
    source_of, receiver = tallies[1:1 + 2 * couples:2], tallies[2:2 + 2 * couples:2]
    slack = jnp.minimum(source_of - 1, most - receiver)
    moved = jax.random.randint(jax.random.fold_in(own_key, 1), (couples,), 0, 1 << 20) % (slack + 1)
    tallies = tallies.at[1:1 + 2 * couples:2].set(source_of - moved).at[2:2 + 2 * couples:2].set(receiver + moved)
    return tallies[jax.random.permutation(jax.random.fold_in(own_key, 2), count)]


def centred(key, shape, spread, bound, pieces=(), held_as=jnp.bfloat16):
    entries = spread * jax.random.normal(key, shape, jnp.float32)
    if pieces:
        entries = entries * steps_of(key, shape, pieces, -0.22, 0.18)
    return jnp.clip(entries, -bound, bound).astype(held_as)


def setup_inputs(seed: int = 0) -> dict:
    arg_keys = jax.random.split(jax.random.key(seed), 8)
    known_inverse = centred(arg_keys[0], (NS, NS), 1.0, 6.0, ((0, 16), (1, 8)), jnp.float32)
    factor_sep = centred(arg_keys[1], (NS, WTOT), (NS * ANC // NBLK) ** -0.5, 0.09375, ((0, 16),), jnp.float32)
    factor_pair = centred(arg_keys[2], (WTOT, WTOT), WMOST ** -0.5, 0.25, ((0, 16),), jnp.float32)
    pivot_inverse = centred(arg_keys[3], (WTOT, WTOT), 1.0, 6.0, ((0, 16), (1, 8)), jnp.float32)
    widths = uneven_parts(arg_keys[4], NSUP, WTOT, WMOST, 2).astype(jnp.int32)
    parent_of = draw_parent_of(jax.random.fold_in(arg_keys[7], 71), 0)
    ancestors = choose_distinct(arg_keys[6], NSUP, NBLK, ANC, 6144)
    return {"known_inverse": known_inverse, "factor_sep": factor_sep, "factor_pair": factor_pair, "pivot_inverse": pivot_inverse, "widths": widths, "parent_of": parent_of, "ancestors": ancestors}


exact_mode = lax.Precision.HIGHEST


def plain_dot(left, right):
    return jnp.dot(left, right, precision=exact_mode, preferred_element_type=jnp.float32)


def first_dot(left, right):
    return lax.dot_general(left, right, (((0,), (0,)), ((), ())), precision=exact_mode, preferred_element_type=jnp.float32)


def supernode_tables(widths, parent_of, ancestors):
    position = jnp.arange(WTOT, dtype=jnp.int32)
    width_ends = jnp.cumsum(widths).astype(jnp.int32)
    column_owner = jnp.sum((width_ends[None, :] <= position[:, None]).astype(jnp.int32), axis=1).astype(jnp.int32)
    owner_onehot = column_owner[:, None] == jnp.arange(NSUP, dtype=jnp.int32)[None, :]
    listed = jnp.any(ancestors[:, :, None] == jnp.arange(NBLK, dtype=jnp.int32)[None, None, :], axis=1).astype(jnp.float32)
    column_blocks = plain_dot(owner_onehot.astype(jnp.float32), listed)
    column_parent = jnp.sum(jnp.where(owner_onehot, parent_of[None, :], 0), axis=1).astype(jnp.int32)
    column_upper = column_parent < 0
    return column_owner, column_blocks, column_parent, column_upper


def reference(known_inverse, factor_sep, factor_pair, pivot_inverse, widths, parent_of, ancestors):
    column_owner, column_blocks, column_parent, column_upper = supernode_tables(widths, parent_of, ancestors)
    sep_index = jnp.arange(NS, dtype=jnp.int32)
    block_onehot = ((sep_index // (NS // NBLK))[:, None] == jnp.arange(NBLK, dtype=jnp.int32)[None, :]).astype(jnp.float32)
    sep_factor = factor_sep * plain_dot(block_onehot, column_blocks.T)
    upper_cols = column_upper.astype(jnp.float32)
    lower_cols = 1.0 - upper_cols
    coupling = jnp.where((column_owner[:, None] == column_parent[None, :]) & (~column_upper)[None, :], factor_pair, 0.0)
    matching = column_owner[:, None] == column_owner[None, :]
    upper_factor = sep_factor * upper_cols[None, :]
    lower_factor = sep_factor * lower_cols[None, :]
    product = -first_dot(sep_factor, known_inverse)
    panel_upper = product * upper_cols[:, None]
    upper_block = jnp.where(matching & column_upper[None, :], pivot_inverse - plain_dot(panel_upper, upper_factor), 0.0)
    panel_lower = product * lower_cols[:, None] - first_dot(coupling, panel_upper)
    pair_block = jnp.where(column_owner[:, None] == column_parent[None, :], -(plain_dot(panel_upper, lower_factor) + plain_dot(upper_block, coupling)), 0.0)
    lower_block = jnp.where(matching & (~column_upper)[None, :], pivot_inverse - plain_dot(panel_lower, lower_factor) - first_dot(pair_block, coupling), 0.0)
    return panel_upper + panel_lower, upper_block + lower_block + pair_block
```

```python
import jax
import jax.numpy as jnp
from jax import lax
from jax.sharding import PartitionSpec as P

NS = 12288
WTOT = 1536
NSUP = 8
NBLK = 64
BLK = NS // NBLK
PARTS = 3


mode = lax.Precision.HIGH


def first_dot(left, right):
    return lax.dot_general(
        left, right, (((0,), (0,)), ((), ())), precision=mode, preferred_element_type=jnp.float32
    )


def gray_of(x):
    return x ^ (x >> 1)


def chip_flip(s, bit):
    z, x = s // 4, s % 4
    if bit == "z":
        return (1 - z) * 4 + x
    return z * 4 + ((x ^ 1) if bit == "a" else (3 - x))


def plane_perm(bit):
    return [(c, chip_flip(c // 2, bit) * 2 + c % 2) for c in range(16)]


def chip_xor_perm(q):
    return [(c, ((c // 2) ^ q) * 2 + c % 2) for c in range(16)]


CORE_PERM = [(c, c ^ 1) for c in range(16)]


def turn_perm(flip):
    out = []
    for r in range(8):
        for c in range(16):
            s, k = c // 2, c % 2
            out.append((r * 16 + c, s * 16 + 2 * r + (k ^ flip)))
    return out


BOTH = ("row", "col")
ORDERS = (("a", "b", "z"), ("b", "z", "a"), ("z", "a", "b"))


def flip_dyn(s, bit):
    z, x = s // 4, s % 4
    if bit == "z":
        return (1 - z) * 4 + x
    return z * 4 + ((x ^ 1) if bit == "a" else (3 - x))


def pick(blocks, index):
    return lax.dynamic_index_in_dim(blocks, index, 0, keepdims=False)


def cube_scatter(value, chip, order):
    blocks = value.reshape(8, -1, value.shape[1])
    d1, d2, d3 = order
    keep = [chip, flip_dyn(chip, d3)]
    keep = keep + [flip_dyn(t, d2) for t in keep]
    give = [flip_dyn(t, d1) for t in keep]
    sent = jnp.stack([pick(blocks, t) for t in give])
    got = lax.ppermute(sent, "col", plane_perm(d1))
    near = jnp.stack([pick(blocks, keep[i]) + got[i] for i in (0, 1)])
    far = jnp.stack([pick(blocks, keep[i]) + got[i] for i in (2, 3)])
    got = lax.ppermute(far, "col", plane_perm(d2))
    last = near[1] + got[1]
    got3 = lax.ppermute(last, "col", plane_perm(d3))
    return near[0] + got[0] + got3


def direct_scatter(blocks, axis, me, perm_of):
    total = pick(blocks, me)
    for q in range(1, 8):
        total = total + lax.ppermute(pick(blocks, me ^ q), axis, perm_of(q))
    return total


def col_scatter(value, chip, core):
    n = value.shape[1]
    pairs = value.reshape(8, 2, -1, n)
    sent = lax.dynamic_index_in_dim(pairs, 1 - core, 1, keepdims=False)
    got = lax.ppermute(sent, "col", CORE_PERM)
    mine = lax.dynamic_index_in_dim(pairs, core, 1, keepdims=False) + got
    return direct_scatter(mine, "col", chip, chip_xor_perm)


def in_order(core, mine, other, axis):
    return jnp.where(
        core == 0,
        jnp.concatenate([mine, other], axis),
        jnp.concatenate([other, mine], axis),
    )


def shards(known_inverse, factor_sep, factor_pair, pivot_inverse, widths, parent_of, ancestors):
    col = lax.axis_index("col")
    row = lax.axis_index("row")
    chip, core = col // 2, col % 2
    position = jnp.arange(WTOT, dtype=jnp.int32)
    lower_tri = jnp.arange(NSUP)[:, None] >= jnp.arange(NSUP)[None, :]
    ends = jnp.sum(jnp.where(lower_tri, widths[None, :], 0), axis=1)
    owner = jnp.sum((ends[:, None] <= position[None, :]).astype(jnp.int32), axis=0)
    owner_is = owner[None, :] == jnp.arange(NSUP, dtype=jnp.int32)[:, None]
    parent = jnp.sum(jnp.where(owner_is, parent_of[:, None], 0), axis=0)
    upper = parent < 0

    blocks_here = NS // 16 // BLK
    block_ids = col * blocks_here + jnp.arange(blocks_here, dtype=jnp.int32)
    listed = jnp.any(ancestors[:, None, :] == block_ids[None, :, None], axis=2)
    column_listed = jnp.any(owner_is[:, None, :] & listed[:, :, None], axis=0)
    factor = jnp.where(
        column_listed[:, None, :], factor_sep.reshape(blocks_here, BLK, WTOT), 0.0
    ).reshape(-1, WTOT)

    def cut(vector, start, size):
        return lax.dynamic_slice_in_dim(vector, start, size)

    owner96 = cut(owner, col * 96, 96)
    coupling = jnp.where((owner96[:, None] == parent[None, :]) & (~upper)[None, :], factor_pair, 0.0)
    coupling_other = lax.ppermute(coupling, "col", CORE_PERM)
    coupling_chip = in_order(core, coupling, coupling_other, 0)
    coupling_t0 = lax.ppermute(coupling, BOTH, turn_perm(0))
    coupling_t1 = lax.ppermute(coupling, BOTH, turn_perm(1))
    coupling_row = in_order(core, coupling_t0, coupling_t1, 0)

    pivot_t = pivot_inverse.T.reshape(2, 96, 96)
    pivot0 = lax.ppermute(pick(pivot_t, core), BOTH, turn_perm(0))
    pivot1 = lax.ppermute(pick(pivot_t, 1 - core), BOTH, turn_perm(1))
    pivot_turned = in_order(core, pivot0, pivot1, 1)

    half = known_inverse.shape[1] // 2
    wide = half // PARTS

    def known_part(which, i):
        return lax.dynamic_slice_in_dim(known_inverse, which * half + i * wide, wide, 1)

    folded = []
    for i in range(PARTS):
        away = first_dot(factor, known_part(1 - core, i))
        folded.append(lax.ppermute(away, "col", CORE_PERM))
    rows = []
    turned = []
    for i in range(PARTS):
        full = first_dot(factor, known_part(core, i)) + folded[i]
        piece = cube_scatter(full, chip, ORDERS[i])
        rows.append(piece)
        turned.append(lax.ppermute(piece, BOTH, turn_perm(0)))

    prod_t = None
    for i in range(PARTS):
        term = lax.dot_general(
            factor[i * wide : (i + 1) * wide],
            turned[i],
            (((0,), (1,)), ((), ())),
            precision=mode,
            preferred_element_type=jnp.float32,
        )
        prod_t = term if prod_t is None else prod_t + term
    prod_t = col_scatter(prod_t, chip, core)

    owner_r = cut(owner, row * 192, 192)
    parent_r = cut(parent, row * 192, 192)
    parent_c = cut(parent, col * 96, 96)
    upper_c = parent_c < 0
    upper_r = parent_r < 0
    own = owner96[:, None] == owner_r[None, :]
    own_upper = own & upper_c[:, None]
    own_lower = own & (~upper_c)[:, None]
    child = parent_c[:, None] == owner_r[None, :]

    base_t = pivot_turned + prod_t
    upper_t = jnp.where(own_upper, base_t, 0.0)
    pair_t = col_scatter(first_dot(coupling, upper_t), chip, core)
    rest_t = jnp.where(child, prod_t - pair_t, 0.0)
    cross_t = jnp.where(child, prod_t, 0.0)
    both_t = jnp.concatenate([rest_t, cross_t], 0)
    mixed = lax.dot_general(
        coupling_row,
        both_t,
        (((0,), (1,)), ((), ())),
        precision=mode,
        preferred_element_type=jnp.float32,
    )
    mixed = direct_scatter(
        mixed.reshape(8, 192, 192), "row", row, lambda q: [(r, r ^ q) for r in range(8)]
    )
    own_lower_turned = own_lower.T
    done = (upper_t + rest_t + jnp.where(own_lower, base_t, 0.0)).T
    done = done - jnp.where(own_lower_turned, mixed[:, 96:], 0.0)
    done = done.reshape(2, 96, 96)
    done0 = lax.ppermute(pick(done, core), BOTH, turn_perm(0))
    done1 = lax.ppermute(pick(done, 1 - core), BOTH, turn_perm(1))
    block = in_order(core, done0, done1, 1) - jnp.where(own_lower, mixed[:, :96].T, 0.0)

    panel = []
    for i in range(PARTS):
        moved = first_dot(coupling_chip, rows[i])
        panel.append(cube_scatter(moved, chip, ORDERS[i]) - rows[i])
    panel = jnp.concatenate(panel, 1).reshape(2, 96, half)
    panel_other = lax.ppermute(pick(panel, 1 - core), "col", CORE_PERM)
    panel = in_order(core, pick(panel, core), panel_other, 1)
    return panel, block


def solution(mesh):
    in_specs = (P("col", "row"), P("col", None), P("col", None), P("col", "row"), P(), P(), P())
    out_specs = (P("col", "row"), P("col", "row"))
    return jax.shard_map(shards, mesh=mesh, in_specs=in_specs, out_specs=out_specs, check_vma=False)
```

```python
import jax
import jax.numpy as jnp
from jax import lax
from jax.experimental import pallas as pl
from jax.experimental.pallas import tpu as pltpu
from jax.sharding import PartitionSpec as P

NS = 12288
WTOT = 1536
NSUP = 8
NBLK = 64
BLK = NS // NBLK
PARTS = 3


def split(x):
    high = x.astype(jnp.bfloat16)
    return high, (x - high.astype(jnp.float32)).astype(jnp.bfloat16)


def mxu(left, right, dims):
    return lax.dot_general(left, right, (dims, ((), ())), preferred_element_type=jnp.float32)


def split_dot(left, right, dims):
    (lh, ll), (rh, rl) = left, right
    return mxu(lh, rh, dims) + (mxu(ll, rh, dims) + mxu(lh, rl, dims))


def lead_kernel(listed, value, high, low):
    x = value[...]
    n = x.shape[0] // listed.shape[0]
    x = jnp.concatenate(
        [
            jnp.where(listed[b : b + 1, :] > 0.0, x[b * n : (b + 1) * n], 0.0)
            for b in range(listed.shape[0])
        ],
        0,
    )
    high[...], low[...] = split(x.T)


def lead_terms(listed, value):
    rows, cols = value.shape
    return pl.pallas_call(
        lead_kernel,
        grid=(cols // 128,),
        in_specs=[
            pl.BlockSpec((listed.shape[0], 128), lambda i: (0, i)),
            pl.BlockSpec((rows, 128), lambda i: (0, i)),
        ],
        out_specs=[pl.BlockSpec((128, rows), lambda i: (i, 0))] * 2,
        out_shape=[jax.ShapeDtypeStruct((cols, rows), jnp.bfloat16)] * 2,
        name="lead_terms",
    )(listed, value)


def product_kernel(which, high, low, known, out):
    right = split(known[...])
    step = 384
    for m in range(0, out.shape[0], step):
        left = (high[m : m + step, :], low[m : m + step, :])
        out[m : m + step, :] = split_dot(left, right, ((1,), (0,)))


def product(which, high, low, known):
    cols, rows = high.shape
    half = known.shape[1] // 2
    wide = half // PARTS
    return pl.pallas_call(
        product_kernel,
        grid_spec=pltpu.PrefetchScalarGridSpec(
            num_scalar_prefetch=1,
            grid=(PARTS,),
            in_specs=[
                pl.BlockSpec((cols, rows), lambda i, w: (0, 0)),
                pl.BlockSpec((cols, rows), lambda i, w: (0, 0)),
                pl.BlockSpec((rows, wide), lambda i, w: (0, w[0] * PARTS + i)),
            ],
            out_specs=pl.BlockSpec((cols, wide), lambda i, w: (0, i)),
        ),
        out_shape=jax.ShapeDtypeStruct((cols, half), jnp.float32),
        name="product",
    )(which.reshape(1), high, low, known)


def turned_kernel(high, low, right, out):
    out[...] = split_dot((high[...], low[...]), split(right[...]), ((1,), (1,)))


def turned_product(high, low, right):
    return pl.pallas_call(
        turned_kernel,
        out_shape=jax.ShapeDtypeStruct((high.shape[0], right.shape[0]), jnp.float32),
        name="turned_product",
    )(high, low, right)


def small_dot(left, right, right_dim):
    def kernel(l, r, out):
        out[...] = split_dot(split(l[...].T), split(r[...]), ((1,), (right_dim,)))

    return pl.pallas_call(
        kernel,
        out_shape=jax.ShapeDtypeStruct((left.shape[1], right.shape[1 - right_dim]), jnp.float32),
        name="small_dot",
    )(left, right)


def chip_flip(s, bit):
    z, x = s // 4, s % 4
    if bit == "z":
        return (1 - z) * 4 + x
    return z * 4 + ((x ^ 1) if bit == "a" else (3 - x))


def plane_perm(bit):
    return [(c, chip_flip(c // 2, bit) * 2 + c % 2) for c in range(16)]


def chip_xor_perm(q):
    return [(c, ((c // 2) ^ q) * 2 + c % 2) for c in range(16)]


CORE_PERM = [(c, c ^ 1) for c in range(16)]


def turn_perm(flip):
    out = []
    for r in range(8):
        for c in range(16):
            s, k = c // 2, c % 2
            out.append((r * 16 + c, s * 16 + 2 * r + (k ^ flip)))
    return out


BOTH = ("row", "col")
ORDERS = (("a", "b", "z"), ("b", "z", "a"), ("z", "a", "b"))


def flip_dyn(s, bit):
    z, x = s // 4, s % 4
    if bit == "z":
        return (1 - z) * 4 + x
    return z * 4 + ((x ^ 1) if bit == "a" else (3 - x))


def pick(blocks, index):
    return lax.dynamic_index_in_dim(blocks, index, 0, keepdims=False)


def cube_scatter(terms, chip, order, hold=None):
    terms = [t.reshape(8, -1, t.shape[1]) for t in terms]

    def block(index):
        return sum(pick(t, index) for t in terms)

    d1, d2, d3 = order
    keep = [chip, flip_dyn(chip, d3)]
    keep = keep + [flip_dyn(t, d2) for t in keep]
    give = [flip_dyn(t, d1) for t in keep]
    sent = jnp.stack([block(t) for t in give])
    got = lax.ppermute(sent, "col", plane_perm(d1))
    near = jnp.stack([block(keep[i]) + got[i] for i in (0, 1)])
    far = jnp.stack([block(keep[i]) + got[i] for i in (2, 3)])
    got = lax.ppermute(far, "col", plane_perm(d2))
    last = near[1] + got[1]
    got3 = lax.ppermute(last, "col", plane_perm(d3))
    return near[0] + got[0] + got3, sent


def direct_scatter(blocks, axis, me, perm_of):
    total = pick(blocks, me)
    for q in range(1, 8):
        total = total + lax.ppermute(pick(blocks, me ^ q), axis, perm_of(q))
    return total


def col_scatter(value, chip, core):
    n = value.shape[1]
    pairs = value.reshape(8, 2, -1, n)
    sent = lax.dynamic_index_in_dim(pairs, 1 - core, 1, keepdims=False)
    got = lax.ppermute(sent, "col", CORE_PERM)
    mine = lax.dynamic_index_in_dim(pairs, core, 1, keepdims=False) + got
    return direct_scatter(mine, "col", chip, chip_xor_perm)


def in_order(core, mine, other, axis):
    return jnp.where(
        core == 0,
        jnp.concatenate([mine, other], axis),
        jnp.concatenate([other, mine], axis),
    )


def shards(known_inverse, factor_sep, factor_pair, pivot_inverse, widths, parent_of, ancestors):
    col = lax.axis_index("col")
    row = lax.axis_index("row")
    chip, core = col // 2, col % 2
    position = jnp.arange(WTOT, dtype=jnp.int32)
    lower_tri = jnp.arange(NSUP)[:, None] >= jnp.arange(NSUP)[None, :]
    ends = jnp.sum(jnp.where(lower_tri, widths[None, :], 0), axis=1)
    owner = jnp.sum((ends[:, None] <= position[None, :]).astype(jnp.int32), axis=0)
    owner_is = owner[None, :] == jnp.arange(NSUP, dtype=jnp.int32)[:, None]
    parent = jnp.sum(jnp.where(owner_is, parent_of[:, None], 0), axis=0)
    upper = parent < 0

    blocks_here = NS // 16 // BLK
    block_ids = col * blocks_here + jnp.arange(blocks_here, dtype=jnp.int32)
    listed = jnp.any(ancestors[:, None, :] == block_ids[None, :, None], axis=2)
    column_listed = jnp.any(owner_is[:, None, :] & listed[:, :, None], axis=0)
    high, low = lead_terms(column_listed.astype(jnp.float32), factor_sep)

    half = known_inverse.shape[1] // 2
    wide = half // PARTS
    away = product(1 - core, high, low, known_inverse)
    folded = lax.ppermute(away, "col", CORE_PERM)
    near = product(core, high, low, known_inverse)
    rows = []
    for i in range(PARTS):
        cut_out = [t[:, i * wide : (i + 1) * wide] for t in (near, folded)]
        piece, sent = cube_scatter(cut_out, chip, ORDERS[i])
        rows.append(piece)
    rows = jnp.concatenate(rows, 1)
    turned = lax.ppermute(rows, BOTH, turn_perm(0))

    def cut(vector, start, size):
        return lax.dynamic_slice_in_dim(vector, start, size)

    pair_in, pivot_in, sent = lax.optimization_barrier((factor_pair, pivot_inverse, sent))
    owner96 = cut(owner, col * 96, 96)
    coupling = jnp.where((owner96[:, None] == parent[None, :]) & (~upper)[None, :], pair_in, 0.0)
    coupling_other = lax.ppermute(coupling, "col", CORE_PERM)
    coupling_chip = in_order(core, coupling, coupling_other, 0)
    pivot_t = pivot_in.T.reshape(2, 96, 96)
    pivot_t = jnp.pad(pivot_t, ((0, 0), (0, 0), (0, 32)))
    turn0 = lax.ppermute(
        jnp.concatenate([coupling, pick(pivot_t, core)], 1), BOTH, turn_perm(0)
    )
    turn1 = lax.ppermute(
        jnp.concatenate([coupling, pick(pivot_t, 1 - core)], 1), BOTH, turn_perm(1)
    )
    coupling_row = in_order(core, turn0[:, :WTOT], turn1[:, :WTOT], 0)
    pivot_turned = in_order(core, turn0[:, WTOT : WTOT + 96], turn1[:, WTOT : WTOT + 96], 1)

    prod_t = turned_product(high, low, turned)
    prod_t = col_scatter(prod_t, chip, core)

    owner_r = cut(owner, row * 192, 192)
    parent_r = cut(parent, row * 192, 192)
    parent_c = cut(parent, col * 96, 96)
    upper_c = parent_c < 0
    upper_r = parent_r < 0
    own = owner96[:, None] == owner_r[None, :]
    own_upper = own & upper_c[:, None]
    own_lower = own & (~upper_c)[:, None]
    child = parent_c[:, None] == owner_r[None, :]

    base_t = pivot_turned + prod_t
    upper_t = jnp.where(own_upper, base_t, 0.0)
    pair_t = col_scatter(small_dot(coupling, upper_t, 0), chip, core)
    rest_t = jnp.where(child, prod_t - pair_t, 0.0)
    cross_t = jnp.where(child, prod_t, 0.0)
    both_t = jnp.concatenate([rest_t, cross_t], 0)
    mixed = small_dot(coupling_row, both_t, 1)
    mixed = direct_scatter(
        mixed.reshape(8, 192, 192), "row", row, lambda q: [(r, r ^ q) for r in range(8)]
    )
    own_lower_turned = own_lower.T
    done = (upper_t + rest_t + jnp.where(own_lower, base_t, 0.0)).T
    done = done - jnp.where(own_lower_turned, mixed[:, 96:], 0.0)
    done = done.reshape(2, 96, 96)
    done0 = lax.ppermute(pick(done, core), BOTH, turn_perm(0))
    done1 = lax.ppermute(pick(done, 1 - core), BOTH, turn_perm(1))
    block = in_order(core, done0, done1, 1) - jnp.where(own_lower, mixed[:, :96].T, 0.0)

    moved = small_dot(coupling_chip, rows, 0)
    panel = []
    for i in range(PARTS):
        piece, _ = cube_scatter([moved[:, i * wide : (i + 1) * wide]], chip, ORDERS[i])
        panel.append(piece)
    panel = (jnp.concatenate(panel, 1) - rows).reshape(2, 96, half)
    panel_other = lax.ppermute(pick(panel, 1 - core), "col", CORE_PERM)
    panel = in_order(core, pick(panel, core), panel_other, 1)
    return panel, block


def solution(mesh):
    in_specs = (P("col", "row"), P("col", None), P("col", None), P("col", "row"), P(), P(), P())
    out_specs = (P("col", "row"), P("col", "row"))
    return jax.shard_map(shards, mesh=mesh, in_specs=in_specs, out_specs=out_specs, check_vma=False)
```

```python
import jax
import jax.numpy as jnp
from jax import lax
from jax.experimental import pallas as pl
from jax.experimental.pallas import tpu as pltpu
from jax.sharding import PartitionSpec as P

NS = 12288
WTOT = 1536
NSUP = 8
NBLK = 64
BLK = NS // NBLK
PARTS = 3
LEAD = 384
TALL = 384
TILE = 256


def split(x):
    high = x.astype(jnp.bfloat16)
    return high, (x - high.astype(jnp.float32)).astype(jnp.bfloat16)


def mxu(left, right, dims):
    return lax.dot_general(left, right, (dims, ((), ())), preferred_element_type=jnp.float32)


def split_dot(left, right, dims):
    (lh, ll), (rh, rl) = left, right
    return mxu(lh, rh, dims) + (mxu(ll, rh, dims) + mxu(lh, rl, dims))


def lead_kernel(listed, value, high, low):
    x = value[...]
    n = x.shape[0] // listed.shape[0]
    x = jnp.concatenate(
        [
            jnp.where(listed[b : b + 1, :] > 0.0, x[b * n : (b + 1) * n], 0.0)
            for b in range(listed.shape[0])
        ],
        0,
    )
    high[...], low[...] = split(x.T)


def lead_terms(listed, value):
    rows, cols = value.shape
    return pl.pallas_call(
        lead_kernel,
        grid=(cols // LEAD,),
        in_specs=[
            pl.BlockSpec((listed.shape[0], LEAD), lambda i: (0, i)),
            pl.BlockSpec((rows, LEAD), lambda i: (0, i)),
        ],
        out_specs=[pl.BlockSpec((LEAD, rows), lambda i: (i, 0))] * 2,
        out_shape=[jax.ShapeDtypeStruct((cols, rows), jnp.bfloat16)] * 2,
        name="lead_terms",
    )(listed, value)


def product_kernel(which, high, low, known, out, known_high, known_low):
    @pl.when(pl.program_id(0) == 0)
    def _():
        known_high[...], known_low[...] = split(known[...])

    right = (known_high[...], known_low[...])
    out[...] = split_dot((high[...], low[...]), right, ((1,), (0,)))


def product(which, high, low, known):
    cols, rows = high.shape
    half = known.shape[1] // 2
    return pl.pallas_call(
        product_kernel,
        grid_spec=pltpu.PrefetchScalarGridSpec(
            num_scalar_prefetch=1,
            grid=(cols // TALL,),
            in_specs=[
                pl.BlockSpec((TALL, rows), lambda i, w: (i, 0)),
                pl.BlockSpec((TALL, rows), lambda i, w: (i, 0)),
                pl.BlockSpec((rows, half), lambda i, w: (0, w[0])),
            ],
            out_specs=pl.BlockSpec((TALL, half), lambda i, w: (i, 0)),
            scratch_shapes=[pltpu.VMEM((rows, half), jnp.bfloat16)] * 2,
        ),
        out_shape=jax.ShapeDtypeStruct((cols, half), jnp.float32),
        name="product",
    )(which.reshape(1), high, low, known)


def pair_kernel(places, owner, parent, *refs):
    pieces, (high, low) = refs[:-2], refs[-2:]
    first_core = places[PARTS * 8] == 0
    stacked = []
    for chip in range(2):
        mine = jnp.concatenate([pieces[(p * 2 + chip) * 2][0] for p in range(PARTS)], 1)
        other = jnp.concatenate([pieces[(p * 2 + chip) * 2 + 1][0] for p in range(PARTS)], 1)
        left = jnp.where(first_core, mine, other)
        right = jnp.where(first_core, other, mine)
        stacked.append(jnp.concatenate([left, right], 1))
    x = jnp.concatenate(stacked, 0)
    x = jnp.where(owner[...] == parent[...], x, 0.0)
    high[...], low[...] = split(x.T)


def pair_terms(places, owner, parent, mine, other):
    rows, wide = mine[0].shape[1:]
    specs, arrays = [], []
    for p in range(PARTS):
        for chip in range(2):
            for array in (mine[p], other[p]):
                specs.append(
                    pl.BlockSpec(
                        (1, rows, wide), lambda i, t, p=p, chip=chip: (t[p * 8 + 2 * i + chip], 0, 0)
                    )
                )
                arrays.append(array)
    return pl.pallas_call(
        pair_kernel,
        grid_spec=pltpu.PrefetchScalarGridSpec(
            num_scalar_prefetch=1,
            grid=(4,),
            in_specs=[
                pl.BlockSpec((2 * rows, 1), lambda i, t: (i, 0)),
                pl.BlockSpec((1, WTOT), lambda i, t: (0, 0)),
            ]
            + specs,
            out_specs=[pl.BlockSpec((WTOT, 2 * rows), lambda i, t: (0, i))] * 2,
        ),
        out_shape=[jax.ShapeDtypeStruct((WTOT, WTOT), jnp.bfloat16)] * 2,
        name="pair_terms",
    )(places, owner[:, None], parent[None, :], *arrays)


def subtract_pairs(flags, pair_high, pair_low, right_high, right_low, out):
    depth = WTOT // 4
    for k in range(4):
        for m in range(WTOT // TILE):

            @pl.when(flags[k * (WTOT // TILE) + m] > 0)
            def _(k=k, m=m):
                at = (slice(m * TILE, (m + 1) * TILE), slice(k * depth, (k + 1) * depth))
                left = (pair_high[at], pair_low[at])
                right = (
                    right_high[k * depth : (k + 1) * depth, :],
                    right_low[k * depth : (k + 1) * depth, :],
                )
                out[at[0], :] = out[at[0], :] - split_dot(left, right, ((1,), (0,)))


def correct_kernel(flags, near, folded, pair_high, pair_low, out, right_high, right_low):
    total = near[...] + folded[...]
    right_high[...], right_low[...] = split(total)
    out[0] = total
    subtract_pairs(flags, pair_high, pair_low, right_high, right_low, out.at[0])


def corrected(flags, near, folded, pair_high, pair_low):
    wide = near.shape[1] // PARTS
    whole = pl.BlockSpec((WTOT, WTOT), lambda i, f: (0, 0))
    return pl.pallas_call(
        correct_kernel,
        grid_spec=pltpu.PrefetchScalarGridSpec(
            num_scalar_prefetch=1,
            grid=(PARTS,),
            in_specs=[pl.BlockSpec((WTOT, wide), lambda i, f: (0, i))] * 2 + [whole, whole],
            out_specs=pl.BlockSpec((1, WTOT, wide), lambda i, f: (i, 0, 0)),
            scratch_shapes=[pltpu.VMEM((WTOT, wide), jnp.bfloat16)] * 2,
        ),
        out_shape=jax.ShapeDtypeStruct((PARTS, WTOT, wide), jnp.float32),
        name="corrected",
    )(flags, near, folded, pair_high, pair_low)


def level_kernel(
    flags, high, low, right, pivot, owner, owner_up, owner_row, pair_high, pair_low, out, rh, rl
):
    out[...] = split_dot((high[...], low[...]), split(right[...]), ((1,), (1,)))
    n = pivot.shape[0]
    start = pl.multiple_of(flags[4 * (WTOT // TILE)] * n, 8)
    own = owner[pl.ds(start, n), :] == owner_row[...]
    out[pl.ds(start, n), :] = out[pl.ds(start, n), :] + jnp.where(own, pivot[...], 0.0)
    rh[...], rl[...] = split(jnp.where(owner_up[...] == owner_row[...], out[...], 0.0))
    subtract_pairs(flags, pair_high, pair_low, rh, rl, out)


def level_terms(flags, high, low, right, pivot, owner, upper, owner_row, pair_high, pair_low):
    wide = right.shape[0]
    owner_up = jnp.where(upper, owner, -1)
    vmem = pl.BlockSpec(memory_space=pltpu.VMEM)
    return pl.pallas_call(
        level_kernel,
        in_specs=[pl.BlockSpec(memory_space=pltpu.SMEM)] + [vmem] * 9,
        out_specs=vmem,
        out_shape=jax.ShapeDtypeStruct((WTOT, wide), jnp.float32),
        scratch_shapes=[pltpu.VMEM((WTOT, wide), jnp.bfloat16)] * 2,
        name="level_terms",
    )(
        flags,
        high,
        low,
        right,
        pivot,
        owner[:, None],
        owner_up[:, None],
        owner_row[None, :],
        pair_high,
        pair_low,
    )


def mixed_kernel(place, pair_high, pair_low, right, out):
    out[...] = split_dot((pair_high[...], pair_low[...]), split(right[...]), ((1,), (1,)))


def mixed_product(place, pair_high, pair_low, right):
    n, depth = right.shape
    return pl.pallas_call(
        mixed_kernel,
        grid_spec=pltpu.PrefetchScalarGridSpec(
            num_scalar_prefetch=1,
            grid=(1,),
            in_specs=[
                pl.BlockSpec((WTOT, depth), lambda i, p: (0, p[0])),
                pl.BlockSpec((WTOT, depth), lambda i, p: (0, p[0])),
                pl.BlockSpec((n, depth), lambda i, p: (0, 0)),
            ],
            out_specs=pl.BlockSpec((WTOT, n), lambda i, p: (0, 0)),
        ),
        out_shape=jax.ShapeDtypeStruct((WTOT, n), jnp.float32),
        name="mixed_product",
    )(place.reshape(1), pair_high, pair_low, right)


def chip_flip(s, bit):
    z, x = s // 4, s % 4
    if bit == "z":
        return (1 - z) * 4 + x
    return z * 4 + ((x ^ 1) if bit == "a" else (3 - x))


def plane_perm(bit):
    return [(c, chip_flip(c // 2, bit) * 2 + c % 2) for c in range(16)]


def chip_xor_perm(q):
    return [(c, ((c // 2) ^ q) * 2 + c % 2) for c in range(16)]


CORE_PERM = [(c, c ^ 1) for c in range(16)]


def turn_perm(flip):
    out = []
    for r in range(8):
        for c in range(16):
            s, k = c // 2, c % 2
            out.append((r * 16 + c, s * 16 + 2 * r + (k ^ flip)))
    return out


BOTH = ("row", "col")
ORDERS = (("a", "b", "z"), ("b", "z", "a"), ("z", "a", "b"))


def flip_dyn(s, bit):
    z, x = s // 4, s % 4
    if bit == "z":
        return (1 - z) * 4 + x
    return z * 4 + ((x ^ 1) if bit == "a" else (3 - x))


def pick(blocks, index):
    return lax.dynamic_index_in_dim(blocks, index, 0, keepdims=False)


def cube_scatter(blocks, chip, order):
    d1, d2, d3 = order
    keep = [chip, flip_dyn(chip, d3)]
    keep = keep + [flip_dyn(t, d2) for t in keep]
    give = [flip_dyn(t, d1) for t in keep]
    got = lax.ppermute(jnp.stack([blocks(t) for t in give]), "col", plane_perm(d1))
    near = jnp.stack([blocks(keep[i]) + got[i] for i in (0, 1)])
    far = jnp.stack([blocks(keep[i]) + got[i] for i in (2, 3)])
    got = lax.ppermute(far, "col", plane_perm(d2))
    last = near[1] + got[1]
    got3 = lax.ppermute(last, "col", plane_perm(d3))
    return near[0] + got[0] + got3


def gray_place(chip, other, order):
    z, x = chip // 4, chip % 4
    zo, xo = other // 4, other % 4
    diff = (x ^ (x >> 1)) ^ (xo ^ (xo >> 1))
    bits = {"a": diff & 1, "b": diff >> 1, "z": z ^ zo}
    return bits[order[0]] + 2 * bits[order[1]] + 4 * bits[order[2]]


def direct_scatter(blocks, axis, me, perm_of):
    total = pick(blocks, me)
    for q in range(1, 8):
        total = total + lax.ppermute(pick(blocks, me ^ q), axis, perm_of(q))
    return total


def col_scatter(value, chip, core):
    n = value.shape[1]
    pairs = value.reshape(8, 2, -1, n)
    sent = lax.dynamic_index_in_dim(pairs, 1 - core, 1, keepdims=False)
    got = lax.ppermute(sent, "col", CORE_PERM)
    mine = lax.dynamic_index_in_dim(pairs, core, 1, keepdims=False) + got
    return direct_scatter(mine, "col", chip, chip_xor_perm)


def in_order(core, mine, other, axis):
    return jnp.where(
        core == 0,
        jnp.concatenate([mine, other], axis),
        jnp.concatenate([other, mine], axis),
    )


def shards(known_inverse, factor_sep, factor_pair, pivot_inverse, widths, parent_of, ancestors):
    col = lax.axis_index("col")
    row = lax.axis_index("row")
    chip, core = col // 2, col % 2
    position = jnp.arange(WTOT, dtype=jnp.int32)
    lower_tri = jnp.arange(NSUP)[:, None] >= jnp.arange(NSUP)[None, :]
    ends = jnp.sum(jnp.where(lower_tri, widths[None, :], 0), axis=1)
    owner = jnp.sum((ends[:, None] <= position[None, :]).astype(jnp.int32), axis=0)
    owner_is = owner[None, :] == jnp.arange(NSUP, dtype=jnp.int32)[:, None]
    parent = jnp.sum(jnp.where(owner_is, parent_of[:, None], 0), axis=0)
    upper = parent < 0

    half = known_inverse.shape[1] // 2
    wide = half // PARTS
    barrier = lax.optimization_barrier

    pair_other = lax.ppermute(factor_pair, "col", CORE_PERM)
    pair_chip = in_order(core, factor_pair, pair_other, 0)
    held = [
        lax.dynamic_slice_in_dim(pair_chip, core * half + p * wide, wide, 1)[None]
        for p in range(PARTS)
    ]

    blocks_here = NS // 16 // BLK
    block_ids = col * blocks_here + jnp.arange(blocks_here, dtype=jnp.int32)
    listed = jnp.any(ancestors[:, None, :] == block_ids[None, :, None], axis=2)
    column_listed = jnp.any(owner_is[:, None, :] & listed[:, :, None], axis=0)

    def gather_step(step):
        return [lax.ppermute(held[p], "col", plane_perm(ORDERS[p][step])) for p in range(PARTS)]

    def grow(got):
        return [jnp.concatenate([a, b], 0) for a, b in zip(held, got)]

    got = gather_step(0)
    listed_f, held = barrier((column_listed.astype(jnp.float32), held))
    high, low = lead_terms(listed_f, factor_sep)
    high, low, got = barrier((high, low, got))
    held = grow(got)
    got = gather_step(1)
    high, low, held = barrier((high, low, held))
    away = product(1 - core, high, low, known_inverse)
    folded = lax.ppermute(away, "col", CORE_PERM)
    away, got = barrier((away, got))
    held = grow(got)
    got = gather_step(2)
    high, low, held = barrier((high, low, held))
    near = product(core, high, low, known_inverse)

    pivot_in, near = barrier((pivot_inverse, near))
    pivot_t = pivot_in.T.reshape(2, 96, 96)
    pivot0 = lax.ppermute(pick(pivot_t, core), BOTH, turn_perm(0))
    pivot1 = lax.ppermute(pick(pivot_t, 1 - core), BOTH, turn_perm(1))

    held = grow(got)
    others = [lax.ppermute(t, "col", CORE_PERM) for t in held]
    places = [gray_place(chip, t, order) for order in ORDERS for t in range(8)]
    places = jnp.stack(places + [core]).astype(jnp.int32)
    pair_high, pair_low = pair_terms(places, owner, parent, held, others)

    row_holds = jnp.any(owner_is.reshape(NSUP, 4, -1), axis=2)
    parent_is = parent[None, :] == jnp.arange(NSUP, dtype=jnp.int32)[:, None]
    col_holds = jnp.any(parent_is.reshape(NSUP, WTOT // TILE, -1), axis=2)
    flags = jnp.any(row_holds[:, :, None] & col_holds[:, None, :], axis=0)
    flags = jnp.concatenate([flags.reshape(-1).astype(jnp.int32), col.astype(jnp.int32)[None]])

    total = corrected(flags, near, folded, pair_high, pair_low).reshape(PARTS * 8, -1, wide)
    rows = []
    for i in range(PARTS):
        rows.append(cube_scatter(lambda t, i=i: pick(total, i * 8 + t), chip, ORDERS[i]))
    rows = jnp.concatenate(rows, 1)
    turned = lax.ppermute(rows, BOTH, turn_perm(0))

    panel = rows.reshape(2, 96, half)
    panel_other = lax.ppermute(pick(panel, 1 - core), "col", CORE_PERM)
    panel = -in_order(core, pick(panel, core), panel_other, 1)

    def cut(vector, start, size):
        return lax.dynamic_slice_in_dim(vector, start, size)

    owner_c = cut(owner, col * 96, 96)
    owner_r = cut(owner, row * 192, 192)
    parent_c = cut(parent, col * 96, 96)
    own = owner_c[:, None] == owner_r[None, :]
    own_lower = own & (parent_c >= 0)[:, None]
    child = parent_c[:, None] == owner_r[None, :]

    pivot_turned = in_order(core, pivot0, pivot1, 1)
    level = level_terms(
        flags, high, low, turned, pivot_turned, owner, upper, owner_r, pair_high, pair_low
    )
    level = col_scatter(level, chip, core)
    pair_t = jnp.where(child, level, 0.0)
    padded = jnp.where(
        row % 2 == 0,
        jnp.pad(pair_t, ((0, 0), (0, 192))),
        jnp.pad(pair_t, ((0, 0), (192, 0))),
    )
    mixed = mixed_product(row // 2, pair_high, pair_low, padded)
    done = jnp.where(own | child, level, 0.0).T.reshape(2, 96, 96)
    mixed = direct_scatter(
        mixed.reshape(8, 192, 96), "row", row, lambda q: [(r, r ^ q) for r in range(8)]
    )
    done0 = lax.ppermute(pick(done, core), BOTH, turn_perm(0))
    done1 = lax.ppermute(pick(done, 1 - core), BOTH, turn_perm(1))
    block = in_order(core, done0, done1, 1) - jnp.where(own_lower, mixed.T, 0.0)
    return panel, block


def solution(mesh):
    in_specs = (P("col", "row"), P("col", None), P("col", None), P("col", "row"), P(), P(), P())
    out_specs = (P("col", "row"), P("col", "row"))
    return jax.shard_map(shards, mesh=mesh, in_specs=in_specs, out_specs=out_specs, check_vma=False)
```

```python
import jax
import jax.numpy as jnp
from jax import lax
from jax.experimental import pallas as pl
from jax.experimental.pallas import tpu as pltpu
from jax.sharding import PartitionSpec as P


NS = 12288
WTOT = 1536
NSUP = 8
NBLK = 64
BLK = NS // NBLK
PARTS = 3
LEAD = 384
TALL = 384
TILE = 256


def split(x):
    high = x.astype(jnp.bfloat16)
    return high, (x - high.astype(jnp.float32)).astype(jnp.bfloat16)


def mxu(left, right, dims):
    return lax.dot_general(left, right, (dims, ((), ())), preferred_element_type=jnp.float32)


def split_dot(left, right, dims):
    (lh, ll), (rh, rl) = left, right
    return mxu(lh, rh, dims) + (mxu(ll, rh, dims) + mxu(lh, rl, dims))


def lead_kernel(listed, value, high, low):
    x = value[...]
    n = x.shape[0] // listed.shape[0]
    x = jnp.concatenate(
        [
            jnp.where(listed[b : b + 1, :] > 0.0, x[b * n : (b + 1) * n], 0.0)
            for b in range(listed.shape[0])
        ],
        0,
    )
    high[...], low[...] = split(x.T)


def lead_terms(listed, value):
    rows, cols = value.shape
    return pl.pallas_call(
        lead_kernel,
        grid=(cols // LEAD,),
        in_specs=[
            pl.BlockSpec((listed.shape[0], LEAD), lambda i: (0, i)),
            pl.BlockSpec((rows, LEAD), lambda i: (0, i)),
        ],
        out_specs=[pl.BlockSpec((LEAD, rows), lambda i: (i, 0))] * 2,
        out_shape=[jax.ShapeDtypeStruct((cols, rows), jnp.bfloat16)] * 2,
        name="lead_terms",
        compiler_params=pltpu.CompilerParams(vmem_limit_bytes=14 << 20),
    )(listed, value)


def product_kernel(which, high, low, known, out, known_high, known_low):
    @pl.when(pl.program_id(0) == 0)
    def _():
        known_high[...], known_low[...] = split(known[...])

    right = (known_high[...], known_low[...])
    out[...] = split_dot((high[...], low[...]), right, ((1,), (0,)))


def product(which, high, low, known):
    cols, rows = high.shape
    half = known.shape[1] // 2
    return pl.pallas_call(
        product_kernel,
        grid_spec=pltpu.PrefetchScalarGridSpec(
            num_scalar_prefetch=1,
            grid=(cols // TALL,),
            in_specs=[
                pl.BlockSpec((TALL, rows), lambda i, w: (i, 0)),
                pl.BlockSpec((TALL, rows), lambda i, w: (i, 0)),
                pl.BlockSpec((rows, half), lambda i, w: (0, w[0])),
            ],
            out_specs=pl.BlockSpec((TALL, half), lambda i, w: (i, 0)),
            scratch_shapes=[pltpu.VMEM((rows, half), jnp.bfloat16)] * 2,
        ),
        out_shape=jax.ShapeDtypeStruct((cols, half), jnp.float32),
        name="product",
        compiler_params=pltpu.CompilerParams(vmem_limit_bytes=18 << 20),
    )(which.reshape(1), high, low, known)


def pair_kernel(places, owner, parent, *refs):
    pieces, (high, low) = refs[:-2], refs[-2:]
    first_core = places[PARTS * 8] == 0
    stacked = []
    for chip in range(2):
        mine = jnp.concatenate([pieces[(p * 2 + chip) * 2][0] for p in range(PARTS)], 1)
        other = jnp.concatenate([pieces[(p * 2 + chip) * 2 + 1][0] for p in range(PARTS)], 1)
        left = jnp.where(first_core, mine, other)
        right = jnp.where(first_core, other, mine)
        stacked.append(jnp.concatenate([left, right], 1))
    x = jnp.concatenate(stacked, 0)
    x = jnp.where(owner[...] == parent[...], x, 0.0)
    high[...], low[...] = split(x.T)


def pair_terms(places, owner, parent, mine, other):
    rows, wide = mine[0].shape[1:]
    specs, arrays = [], []
    for p in range(PARTS):
        for chip in range(2):
            for array in (mine[p], other[p]):
                specs.append(
                    pl.BlockSpec(
                        (1, rows, wide), lambda i, t, p=p, chip=chip: (t[p * 8 + 2 * i + chip], 0, 0)
                    )
                )
                arrays.append(array)
    return pl.pallas_call(
        pair_kernel,
        grid_spec=pltpu.PrefetchScalarGridSpec(
            num_scalar_prefetch=1,
            grid=(4,),
            in_specs=[
                pl.BlockSpec((2 * rows, 1), lambda i, t: (i, 0)),
                pl.BlockSpec((1, WTOT), lambda i, t: (0, 0)),
            ]
            + specs,
            out_specs=[pl.BlockSpec((WTOT, 2 * rows), lambda i, t: (0, i))] * 2,
        ),
        out_shape=[jax.ShapeDtypeStruct((WTOT, WTOT), jnp.bfloat16)] * 2,
        name="pair_terms",
        compiler_params=pltpu.CompilerParams(vmem_limit_bytes=24 << 20),
    )(places, owner[:, None], parent[None, :], *arrays)


def subtract_pairs(flags, pair_high, pair_low, right_high, right_low, out):
    depth = WTOT // 4
    for k in range(4):
        for m in range(WTOT // TILE):

            @pl.when(flags[k * (WTOT // TILE) + m] > 0)
            def _(k=k, m=m):
                at = (slice(m * TILE, (m + 1) * TILE), slice(k * depth, (k + 1) * depth))
                left = (pair_high[at], pair_low[at])
                right = (
                    right_high[k * depth : (k + 1) * depth, :],
                    right_low[k * depth : (k + 1) * depth, :],
                )
                out[at[0], :] = out[at[0], :] - split_dot(left, right, ((1,), (0,)))


def correct_kernel(flags, near, folded, pair_high, pair_low, out, right_high, right_low):
    total = near[...] + folded[...]
    right_high[...], right_low[...] = split(total)
    out[0] = total
    subtract_pairs(flags, pair_high, pair_low, right_high, right_low, out.at[0])


def corrected(flags, near, folded, pair_high, pair_low):
    wide = near.shape[1] // PARTS
    whole = pl.BlockSpec((WTOT, WTOT), lambda i, f: (0, 0), pipeline_mode=pl.Buffered(1))
    return pl.pallas_call(
        correct_kernel,
        grid_spec=pltpu.PrefetchScalarGridSpec(
            num_scalar_prefetch=1,
            grid=(PARTS,),
            in_specs=[pl.BlockSpec((WTOT, wide), lambda i, f: (0, i))] * 2 + [whole, whole],
            out_specs=pl.BlockSpec((1, WTOT, wide), lambda i, f: (i, 0, 0)),
            scratch_shapes=[pltpu.VMEM((WTOT, wide), jnp.bfloat16)] * 2,
        ),
        out_shape=jax.ShapeDtypeStruct((PARTS, WTOT, wide), jnp.float32),
        name="corrected",
        compiler_params=pltpu.CompilerParams(vmem_limit_bytes=26 << 20),
    )(flags, near, folded, pair_high, pair_low)


def level_kernel(
    flags, high, low, right, pivot, owner, owner_up, owner_row, pair_high, pair_low, out, rh, rl
):
    out[...] = split_dot((high[...], low[...]), split(right[...]), ((1,), (1,)))
    n = pivot.shape[0]
    start = pl.multiple_of(flags[4 * (WTOT // TILE)] * n, 8)
    own = owner[pl.ds(start, n), :] == owner_row[...]
    out[pl.ds(start, n), :] = out[pl.ds(start, n), :] + jnp.where(own, pivot[...], 0.0)
    rh[...], rl[...] = split(jnp.where(owner_up[...] == owner_row[...], out[...], 0.0))
    subtract_pairs(flags, pair_high, pair_low, rh, rl, out)


def level_terms(flags, high, low, right, pivot, owner, upper, owner_row, pair_high, pair_low):
    wide = right.shape[0]
    owner_up = jnp.where(upper, owner, -1)
    vmem = pl.BlockSpec(memory_space=pltpu.VMEM)
    return pl.pallas_call(
        level_kernel,
        in_specs=[pl.BlockSpec(memory_space=pltpu.SMEM)] + [vmem] * 9,
        out_specs=vmem,
        out_shape=jax.ShapeDtypeStruct((WTOT, wide), jnp.float32),
        scratch_shapes=[pltpu.VMEM((WTOT, wide), jnp.bfloat16)] * 2,
        name="level_terms",
        compiler_params=pltpu.CompilerParams(vmem_limit_bytes=26 << 20),
    )(
        flags,
        high,
        low,
        right,
        pivot,
        owner[:, None],
        owner_up[:, None],
        owner_row[None, :],
        pair_high,
        pair_low,
    )


def mixed_kernel(place, pair_high, pair_low, right, out):
    out[...] = split_dot((pair_high[...], pair_low[...]), split(right[...]), ((1,), (1,)))


def mixed_product(place, pair_high, pair_low, right):
    n, depth = right.shape
    return pl.pallas_call(
        mixed_kernel,
        grid_spec=pltpu.PrefetchScalarGridSpec(
            num_scalar_prefetch=1,
            grid=(1,),
            in_specs=[
                pl.BlockSpec((WTOT, depth), lambda i, p: (0, p[0])),
                pl.BlockSpec((WTOT, depth), lambda i, p: (0, p[0])),
                pl.BlockSpec((n, depth), lambda i, p: (0, 0)),
            ],
            out_specs=pl.BlockSpec((WTOT, n), lambda i, p: (0, 0)),
        ),
        out_shape=jax.ShapeDtypeStruct((WTOT, n), jnp.float32),
        name="mixed_product",
        compiler_params=pltpu.CompilerParams(vmem_limit_bytes=12 << 20),
    )(place.reshape(1), pair_high, pair_low, right)


def chip_flip(s, bit):
    z, x = s // 4, s % 4
    if bit == "z":
        return (1 - z) * 4 + x
    return z * 4 + ((x ^ 1) if bit == "a" else (3 - x))


def plane_perm(bit):
    return [(c, chip_flip(c // 2, bit) * 2 + c % 2) for c in range(16)]


def chip_xor_perm(q):
    return [(c, ((c // 2) ^ q) * 2 + c % 2) for c in range(16)]


CORE_PERM = [(c, c ^ 1) for c in range(16)]


def turn_perm(flip):
    out = []
    for r in range(8):
        for c in range(16):
            s, k = c // 2, c % 2
            out.append((r * 16 + c, s * 16 + 2 * r + (k ^ flip)))
    return out


BOTH = ("row", "col")
ORDERS = (("a", "b", "z"), ("b", "z", "a"), ("z", "a", "b"))


def flip_dyn(s, bit):
    z, x = s // 4, s % 4
    if bit == "z":
        return (1 - z) * 4 + x
    return z * 4 + ((x ^ 1) if bit == "a" else (3 - x))


def pick(blocks, index):
    return lax.dynamic_index_in_dim(blocks, index, 0, keepdims=False)


def cube_scatter(blocks, chip, order):
    d1, d2, d3 = order
    keep = [chip, flip_dyn(chip, d3)]
    keep = keep + [flip_dyn(t, d2) for t in keep]
    give = [flip_dyn(t, d1) for t in keep]
    got = lax.ppermute(jnp.stack([blocks(t) for t in give]), "col", plane_perm(d1))
    near = jnp.stack([blocks(keep[i]) + got[i] for i in (0, 1)])
    far = jnp.stack([blocks(keep[i]) + got[i] for i in (2, 3)])
    got = lax.ppermute(far, "col", plane_perm(d2))
    last = near[1] + got[1]
    got3 = lax.ppermute(last, "col", plane_perm(d3))
    return near[0] + got[0] + got3


def gray_place(chip, other, order):
    z, x = chip // 4, chip % 4
    zo, xo = other // 4, other % 4
    diff = (x ^ (x >> 1)) ^ (xo ^ (xo >> 1))
    bits = {"a": diff & 1, "b": diff >> 1, "z": z ^ zo}
    return bits[order[0]] + 2 * bits[order[1]] + 4 * bits[order[2]]


def direct_scatter(blocks, axis, me, perm_of):
    total = pick(blocks, me)
    for q in range(1, 8):
        total = total + lax.ppermute(pick(blocks, me ^ q), axis, perm_of(q))
    return total


def col_scatter(value, chip, core):
    n = value.shape[1]
    pairs = value.reshape(8, 2, -1, n)
    sent = lax.dynamic_index_in_dim(pairs, 1 - core, 1, keepdims=False)
    got = lax.ppermute(sent, "col", CORE_PERM)
    mine = lax.dynamic_index_in_dim(pairs, core, 1, keepdims=False) + got
    return direct_scatter(mine, "col", chip, chip_xor_perm)


def in_order(core, mine, other, axis):
    return jnp.where(
        core == 0,
        jnp.concatenate([mine, other], axis),
        jnp.concatenate([other, mine], axis),
    )


def shards(known_inverse, factor_sep, factor_pair, pivot_inverse, widths, parent_of, ancestors):
    col = lax.axis_index("col")
    row = lax.axis_index("row")
    chip, core = col // 2, col % 2
    position = jnp.arange(WTOT, dtype=jnp.int32)
    lower_tri = jnp.arange(NSUP)[:, None] >= jnp.arange(NSUP)[None, :]
    ends = jnp.sum(jnp.where(lower_tri, widths[None, :], 0), axis=1)
    owner = jnp.sum((ends[:, None] <= position[None, :]).astype(jnp.int32), axis=0)
    owner_is = owner[None, :] == jnp.arange(NSUP, dtype=jnp.int32)[:, None]
    parent = jnp.sum(jnp.where(owner_is, parent_of[:, None], 0), axis=0)
    upper = parent < 0

    half = known_inverse.shape[1] // 2
    wide = half // PARTS
    barrier = lax.optimization_barrier

    pair_other = lax.ppermute(factor_pair, "col", CORE_PERM)
    pair_chip = in_order(core, factor_pair, pair_other, 0)
    held = [
        lax.dynamic_slice_in_dim(pair_chip, core * half + p * wide, wide, 1)[None]
        for p in range(PARTS)
    ]

    blocks_here = NS // 16 // BLK
    block_ids = col * blocks_here + jnp.arange(blocks_here, dtype=jnp.int32)
    listed = jnp.any(ancestors[:, None, :] == block_ids[None, :, None], axis=2)
    column_listed = jnp.any(owner_is[:, None, :] & listed[:, :, None], axis=0)

    def gather_step(step):
        out = []
        for p in range(PARTS):
            out.append(lax.ppermute(held[p], "col", plane_perm(ORDERS[p][step])))
        return out

    def grow(got):
        return [jnp.concatenate([a, b], 0) for a, b in zip(held, got)]

    got = gather_step(0)
    listed_f, held = barrier((column_listed.astype(jnp.float32), held))
    high, low = lead_terms(listed_f, factor_sep)
    high, low, got = barrier((high, low, got))
    held = grow(got)
    got = gather_step(1)
    high, low, held = barrier((high, low, held))
    away = product(1 - core, high, low, known_inverse)
    folded = lax.ppermute(away, "col", CORE_PERM)
    away, got = barrier((away, got))
    held = grow(got)
    got = gather_step(2)
    high, low, held = barrier((high, low, held))
    near = product(core, high, low, known_inverse)

    pivot_got = lax.ppermute(pivot_inverse.T.reshape(2, 96, 96), BOTH, turn_perm(0))
    pivot_other = lax.ppermute(pick(pivot_got, 1 - core), "col", CORE_PERM)
    pivot_turned = in_order(core, pick(pivot_got, core), pivot_other, 1)

    held = grow(got)
    others = []
    for p in range(PARTS):
        others.append(lax.ppermute(held[p], "col", CORE_PERM))
    places = [gray_place(chip, t, order) for order in ORDERS for t in range(8)]
    places = jnp.stack(places + [core]).astype(jnp.int32)
    pair_high, pair_low = pair_terms(places, owner, parent, held, others)

    row_holds = jnp.any(owner_is.reshape(NSUP, 4, -1), axis=2)
    parent_is = parent[None, :] == jnp.arange(NSUP, dtype=jnp.int32)[:, None]
    col_holds = jnp.any(parent_is.reshape(NSUP, WTOT // TILE, -1), axis=2)
    flags = jnp.any(row_holds[:, :, None] & col_holds[:, None, :], axis=0)
    flags = jnp.concatenate([flags.reshape(-1).astype(jnp.int32), col.astype(jnp.int32)[None]])

    total = corrected(flags, near, folded, pair_high, pair_low).reshape(PARTS * 8, -1, wide)
    rows = []
    for i in range(PARTS):
        rows.append(cube_scatter(lambda t, i=i: pick(total, i * 8 + t), chip, ORDERS[i]))
    rows = jnp.concatenate(rows, 1)
    turned = lax.ppermute(rows, BOTH, turn_perm(0))

    panel = rows.reshape(2, 96, half)
    panel_other = lax.ppermute(pick(panel, 1 - core), "col", CORE_PERM)
    panel = -in_order(core, pick(panel, core), panel_other, 1)

    def cut(vector, start, size):
        return lax.dynamic_slice_in_dim(vector, start, size)

    owner_c = cut(owner, col * 96, 96)
    owner_r = cut(owner, row * 192, 192)
    parent_c = cut(parent, col * 96, 96)
    own = owner_c[:, None] == owner_r[None, :]
    own_lower = own & (parent_c >= 0)[:, None]
    child = parent_c[:, None] == owner_r[None, :]

    level = level_terms(
        flags, high, low, turned, pivot_turned, owner, upper, owner_r, pair_high, pair_low
    )
    level = col_scatter(level, chip, core)
    pair_t = jnp.where(child, level, 0.0)
    padded = jnp.where(
        row % 2 == 0,
        jnp.pad(pair_t, ((0, 0), (0, 192))),
        jnp.pad(pair_t, ((0, 0), (192, 0))),
    )
    mixed = mixed_product(row // 2, pair_high, pair_low, padded)
    done = jnp.where(own | child, level, 0.0).T.reshape(2, 96, 96)
    mixed = direct_scatter(
        mixed.reshape(8, 192, 96), "row", row, lambda q: [(r, r ^ q) for r in range(8)]
    )
    done = lax.ppermute(done, BOTH, turn_perm(0))
    done_other = lax.ppermute(pick(done, 1 - core), "col", CORE_PERM)
    block = in_order(core, pick(done, core), done_other, 1) - jnp.where(own_lower, mixed.T, 0.0)
    return panel, block


def solution(mesh):
    in_specs = (P("col", "row"), P("col", None), P("col", None), P("col", "row"), P(), P(), P())
    out_specs = (P("col", "row"), P("col", "row"))

    return jax.shard_map(shards, mesh=mesh, in_specs=in_specs, out_specs=out_specs, check_vma=False)
```

```python
import jax
import jax.numpy as jnp
from jax import lax
from jax.experimental import pallas as pl
from jax.experimental.pallas import tpu as pltpu
from jax.sharding import PartitionSpec as P


NS = 12288
WTOT = 1536
NSUP = 8
NBLK = 64
BLK = NS // NBLK
PARTS = 3
LEAD = 384
TALL = 384
TILE = 256


def split(x):
    high = x.astype(jnp.bfloat16)
    return high, (x - high.astype(jnp.float32)).astype(jnp.bfloat16)


def mxu(left, right, dims):
    return lax.dot_general(left, right, (dims, ((), ())), preferred_element_type=jnp.float32)


def split_dot(left, right, dims):
    (lh, ll), (rh, rl) = left, right
    return mxu(lh, rh, dims) + (mxu(ll, rh, dims) + mxu(lh, rl, dims))


def lead_kernel(listed, value, high, low):
    x = value[...]
    n = x.shape[0] // listed.shape[0]
    x = jnp.concatenate(
        [
            jnp.where(listed[b : b + 1, :] > 0.0, x[b * n : (b + 1) * n], 0.0)
            for b in range(listed.shape[0])
        ],
        0,
    )
    high[...], low[...] = split(x.T)


def lead_terms(listed, value):
    rows, cols = value.shape
    return pl.pallas_call(
        lead_kernel,
        grid=(cols // LEAD,),
        in_specs=[
            pl.BlockSpec((listed.shape[0], LEAD), lambda i: (0, i)),
            pl.BlockSpec((rows, LEAD), lambda i: (0, i)),
        ],
        out_specs=[pl.BlockSpec((LEAD, rows), lambda i: (i, 0))] * 2,
        out_shape=[jax.ShapeDtypeStruct((cols, rows), jnp.bfloat16)] * 2,
        name="lead_terms",
        compiler_params=pltpu.CompilerParams(vmem_limit_bytes=14 << 20),
    )(listed, value)


def product_kernel(which, high, low, known, *refs):
    *added, out, known_high, known_low = refs

    @pl.when(pl.program_id(0) == 0)
    def _():
        known_high[...], known_low[...] = split(known[...])

    right = (known_high[...], known_low[...])
    value = split_dot((high[...], low[...]), right, ((1,), (0,)))
    out[...] = value + added[0][...] if added else value


def product(which, high, low, known, *added):
    cols, rows = high.shape
    half = known.shape[1] // 2
    return pl.pallas_call(
        product_kernel,
        grid_spec=pltpu.PrefetchScalarGridSpec(
            num_scalar_prefetch=1,
            grid=(cols // TALL,),
            in_specs=[
                pl.BlockSpec((TALL, rows), lambda i, w: (i, 0)),
                pl.BlockSpec((TALL, rows), lambda i, w: (i, 0)),
                pl.BlockSpec((rows, half), lambda i, w: (0, w[0])),
            ]
            + [pl.BlockSpec((TALL, half), lambda i, w: (i, 0)) for _ in added],
            out_specs=pl.BlockSpec((TALL, half), lambda i, w: (i, 0)),
            scratch_shapes=[pltpu.VMEM((rows, half), jnp.bfloat16)] * 2,
        ),
        out_shape=jax.ShapeDtypeStruct((cols, half), jnp.float32),
        name="product",
        compiler_params=pltpu.CompilerParams(vmem_limit_bytes=22 << 20),
    )(which.reshape(1), high, low, known, *added)


def pair_kernel(places, owner, parent, *refs):
    pieces, (high, low) = refs[:-2], refs[-2:]
    first_core = places[PARTS * 8] == 0
    stacked = []
    for chip in range(2):
        mine = jnp.concatenate([pieces[(p * 2 + chip) * 2][0] for p in range(PARTS)], 1)
        other = jnp.concatenate([pieces[(p * 2 + chip) * 2 + 1][0] for p in range(PARTS)], 1)
        left = jnp.where(first_core, mine, other)
        right = jnp.where(first_core, other, mine)
        stacked.append(jnp.concatenate([left, right], 1))
    x = jnp.concatenate(stacked, 0)
    x = jnp.where(owner[...] == parent[...], x, 0.0)
    high[...], low[...] = split(x.T)


def pair_terms(places, owner, parent, mine, other):
    rows, wide = mine[0].shape[1:]
    specs, arrays = [], []
    for p in range(PARTS):
        for chip in range(2):
            for array in (mine[p], other[p]):
                specs.append(
                    pl.BlockSpec(
                        (1, rows, wide), lambda i, t, p=p, chip=chip: (t[p * 8 + 2 * i + chip], 0, 0)
                    )
                )
                arrays.append(array)
    return pl.pallas_call(
        pair_kernel,
        grid_spec=pltpu.PrefetchScalarGridSpec(
            num_scalar_prefetch=1,
            grid=(4,),
            in_specs=[
                pl.BlockSpec((2 * rows, 1), lambda i, t: (i, 0)),
                pl.BlockSpec((1, WTOT), lambda i, t: (0, 0)),
            ]
            + specs,
            out_specs=[pl.BlockSpec((WTOT, 2 * rows), lambda i, t: (0, i))] * 2,
        ),
        out_shape=[jax.ShapeDtypeStruct((WTOT, WTOT), jnp.bfloat16)] * 2,
        name="pair_terms",
        compiler_params=pltpu.CompilerParams(vmem_limit_bytes=24 << 20),
    )(places, owner[:, None], parent[None, :], *arrays)


def subtract_pairs(flags, pair_high, pair_low, right_high, right_low, out):
    depth = WTOT // 4
    for k in range(4):
        for m in range(WTOT // TILE):

            @pl.when(flags[k * (WTOT // TILE) + m] > 0)
            def _(k=k, m=m):
                at = (slice(m * TILE, (m + 1) * TILE), slice(k * depth, (k + 1) * depth))
                left = (pair_high[at], pair_low[at])
                right = (
                    right_high[k * depth : (k + 1) * depth, :],
                    right_low[k * depth : (k + 1) * depth, :],
                )
                out[at[0], :] = out[at[0], :] - split_dot(left, right, ((1,), (0,)))


def correct_kernel(flags, total, pair_high, pair_low, out, right_high, right_low, acc):
    m = pl.program_id(0)

    @pl.when(m == 0)
    def _():
        right_high[...], right_low[...] = split(total[...])

    acc[...] = total[pl.ds(pl.multiple_of(m * TILE, TILE), TILE), :]
    depth = WTOT // 4
    for k in range(4):

        @pl.when(flags[k * (WTOT // TILE) + m] > 0)
        def _(k=k):
            at = slice(k * depth, (k + 1) * depth)
            left = (pair_high[:, at], pair_low[:, at])
            acc[...] = acc[...] - split_dot(left, (right_high[at, :], right_low[at, :]), ((1,), (0,)))

    wide = out.shape[2]
    for p in range(out.shape[0]):
        out[p] = acc[:, p * wide : (p + 1) * wide]


def corrected(flags, total, pair_high, pair_low):
    half = total.shape[1]
    wide = half // PARTS
    return pl.pallas_call(
        correct_kernel,
        grid_spec=pltpu.PrefetchScalarGridSpec(
            num_scalar_prefetch=1,
            grid=(WTOT // TILE,),
            in_specs=[
                pl.BlockSpec((WTOT, half), lambda i, f: (0, 0), pipeline_mode=pl.Buffered(1)),
                pl.BlockSpec((TILE, WTOT), lambda i, f: (i, 0)),
                pl.BlockSpec((TILE, WTOT), lambda i, f: (i, 0)),
            ],
            out_specs=pl.BlockSpec((PARTS, TILE, wide), lambda i, f: (0, i, 0)),
            scratch_shapes=[pltpu.VMEM((WTOT, half), jnp.bfloat16)] * 2
            + [pltpu.VMEM((TILE, half), jnp.float32)],
        ),
        out_shape=jax.ShapeDtypeStruct((PARTS, WTOT, wide), jnp.float32),
        name="corrected",
        compiler_params=pltpu.CompilerParams(vmem_limit_bytes=24 << 20),
    )(flags, total, pair_high, pair_low)


def level_kernel(
    flags, high, low, right, pivot, owner, owner_up, owner_row, far_high, far_low, out, rh, rl,
    pair_high, pair_low, arrived
):
    loads = [
        pltpu.make_async_copy(far_high, pair_high, arrived.at[0]),
        pltpu.make_async_copy(far_low, pair_low, arrived.at[1]),
    ]
    for load in loads:
        load.start()
    out[...] = split_dot((high[...], low[...]), split(right[...]), ((1,), (1,)))
    n = pivot.shape[0]
    start = pl.multiple_of(flags[4 * (WTOT // TILE)] * n, 8)
    own = owner[pl.ds(start, n), :] == owner_row[...]
    out[pl.ds(start, n), :] = out[pl.ds(start, n), :] + jnp.where(own, pivot[...], 0.0)
    rh[...], rl[...] = split(jnp.where(owner_up[...] == owner_row[...], out[...], 0.0))
    for load in loads:
        load.wait()
    subtract_pairs(flags, pair_high, pair_low, rh, rl, out)


def level_terms(flags, high, low, right, pivot, owner, upper, owner_row, pair_high, pair_low):
    wide = right.shape[0]
    owner_up = jnp.where(upper, owner, -1)
    vmem = pl.BlockSpec(memory_space=pltpu.VMEM)
    return pl.pallas_call(
        level_kernel,
        in_specs=[pl.BlockSpec(memory_space=pltpu.SMEM)]
        + [vmem] * 7
        + [pl.BlockSpec(memory_space=pl.ANY)] * 2,
        out_specs=vmem,
        out_shape=jax.ShapeDtypeStruct((WTOT, wide), jnp.float32),
        scratch_shapes=[pltpu.VMEM((WTOT, wide), jnp.bfloat16)] * 2
        + [pltpu.VMEM((WTOT, WTOT), jnp.bfloat16)] * 2
        + [pltpu.SemaphoreType.DMA((2,))],
        name="level_terms",
    )(
        flags,
        high,
        low,
        right,
        pivot,
        owner[:, None],
        owner_up[:, None],
        owner_row[None, :],
        pair_high,
        pair_low,
    )


def mixed_kernel(place, pair_high, pair_low, right, out):
    out[...] = split_dot((pair_high[...], pair_low[...]), split(right[...]), ((1,), (1,)))


def mixed_product(place, pair_high, pair_low, right):
    n, depth = right.shape
    return pl.pallas_call(
        mixed_kernel,
        grid_spec=pltpu.PrefetchScalarGridSpec(
            num_scalar_prefetch=1,
            grid=(1,),
            in_specs=[
                pl.BlockSpec((WTOT, depth), lambda i, p: (0, p[0])),
                pl.BlockSpec((WTOT, depth), lambda i, p: (0, p[0])),
                pl.BlockSpec((n, depth), lambda i, p: (0, 0)),
            ],
            out_specs=pl.BlockSpec((WTOT, n), lambda i, p: (0, 0)),
        ),
        out_shape=jax.ShapeDtypeStruct((WTOT, n), jnp.float32),
        name="mixed_product",
    )(place.reshape(1), pair_high, pair_low, right)


def chip_flip(s, bit):
    z, x = s // 4, s % 4
    if bit == "z":
        return (1 - z) * 4 + x
    return z * 4 + ((x ^ 1) if bit == "a" else (3 - x))


def plane_perm(bit):
    return [(c, chip_flip(c // 2, bit) * 2 + c % 2) for c in range(16)]


def chip_xor_perm(q):
    return [(c, ((c // 2) ^ q) * 2 + c % 2) for c in range(16)]


CORE_PERM = [(c, c ^ 1) for c in range(16)]


SIGMA = (0, 2, 4, 6, 1, 3, 5, 7)


def turn_perm():
    return [
        (r * 16 + s * 2 + k, SIGMA[s] * 16 + r * 2 + k)
        for r in range(8)
        for s in range(8)
        for k in range(2)
    ]


def back_perm():
    return [(b, a) for a, b in turn_perm()]


BOTH = ("row", "col")
ORDERS = (("a", "b", "z"), ("b", "z", "a"), ("z", "a", "b"))


def flip_dyn(s, bit):
    z, x = s // 4, s % 4
    if bit == "z":
        return (1 - z) * 4 + x
    return z * 4 + ((x ^ 1) if bit == "a" else (3 - x))


def pick(blocks, index):
    return lax.dynamic_index_in_dim(blocks, index, 0, keepdims=False)


def cube_scatter(blocks, chip, order):
    d1, d2, d3 = order
    keep = [chip, flip_dyn(chip, d3)]
    keep = keep + [flip_dyn(t, d2) for t in keep]
    give = [flip_dyn(t, d1) for t in keep]
    got = lax.ppermute(jnp.stack([blocks(t) for t in give]), "col", plane_perm(d1))
    near = jnp.stack([blocks(keep[i]) + got[i] for i in (0, 1)])
    far = jnp.stack([blocks(keep[i]) + got[i] for i in (2, 3)])
    got = lax.ppermute(far, "col", plane_perm(d2))
    last = near[1] + got[1]
    got3 = lax.ppermute(last, "col", plane_perm(d3))
    return near[0] + got[0] + got3


def gray_place(chip, other, order):
    z, x = chip // 4, chip % 4
    zo, xo = other // 4, other % 4
    diff = (x ^ (x >> 1)) ^ (xo ^ (xo >> 1))
    bits = {"a": diff & 1, "b": diff >> 1, "z": z ^ zo}
    return bits[order[0]] + 2 * bits[order[1]] + 4 * bits[order[2]]


def direct_scatter(blocks, axis, me, perm_of):
    total = pick(blocks, me)
    for q in range(1, 8):
        total = total + lax.ppermute(pick(blocks, me ^ q), axis, perm_of(q))
    return total


def col_scatter(value, chip, core):
    n = value.shape[1]
    pairs = value.reshape(8, 2, -1, n)
    sent = lax.dynamic_index_in_dim(pairs, 1 - core, 1, keepdims=False)
    got = lax.ppermute(sent, "col", CORE_PERM)
    mine = lax.dynamic_index_in_dim(pairs, core, 1, keepdims=False) + got
    return direct_scatter(mine, "col", chip, chip_xor_perm)


def in_order(core, mine, other, axis):
    return jnp.where(
        core == 0,
        jnp.concatenate([mine, other], axis),
        jnp.concatenate([other, mine], axis),
    )


def shards(known_inverse, factor_sep, factor_pair, pivot_inverse, widths, parent_of, ancestors):
    col = lax.axis_index("col")
    row = lax.axis_index("row")
    chip, core = col // 2, col % 2
    position = jnp.arange(WTOT, dtype=jnp.int32)
    lower_tri = jnp.arange(NSUP)[:, None] >= jnp.arange(NSUP)[None, :]
    ends = jnp.sum(jnp.where(lower_tri, widths[None, :], 0), axis=1)
    owner = jnp.sum((ends[:, None] <= position[None, :]).astype(jnp.int32), axis=0)
    owner_is = owner[None, :] == jnp.arange(NSUP, dtype=jnp.int32)[:, None]
    parent = jnp.sum(jnp.where(owner_is, parent_of[:, None], 0), axis=0)
    upper = parent < 0

    half = known_inverse.shape[1] // 2
    wide = half // PARTS
    barrier = lax.optimization_barrier

    pair_other = lax.ppermute(factor_pair, "col", CORE_PERM)
    pair_chip = in_order(core, factor_pair, pair_other, 0)
    held = [
        lax.dynamic_slice_in_dim(pair_chip, core * half + p * wide, wide, 1)[None]
        for p in range(PARTS)
    ]

    blocks_here = NS // 16 // BLK
    block_ids = col * blocks_here + jnp.arange(blocks_here, dtype=jnp.int32)
    listed = jnp.any(ancestors[:, None, :] == block_ids[None, :, None], axis=2)
    column_listed = jnp.any(owner_is[:, None, :] & listed[:, :, None], axis=0)

    def gather_step(step):
        out = []
        for p in range(PARTS):
            out.append(lax.ppermute(held[p], "col", plane_perm(ORDERS[p][step])))
        return out

    def grow(got):
        return [jnp.concatenate([a, b], 0) for a, b in zip(held, got)]

    got = gather_step(0)
    listed_f, held = barrier((column_listed.astype(jnp.float32), held))
    high, low = lead_terms(listed_f, factor_sep)
    high, low, got = barrier((high, low, got))
    held = grow(got)
    got = gather_step(1)
    high, low, held = barrier((high, low, held))
    away = product(1 - core, high, low, known_inverse)
    folded = lax.ppermute(away, "col", CORE_PERM)
    away, got = barrier((away, got))
    held = grow(got)
    got = gather_step(2)
    high, low, held = barrier((high, low, held))
    near = product(core, high, low, known_inverse, folded)

    pivot_got = lax.ppermute(pivot_inverse.T.reshape(2, 96, 96), BOTH, turn_perm())
    pivot_other = lax.ppermute(pick(pivot_got, 1 - core), "col", CORE_PERM)
    pivot_turned = in_order(core, pick(pivot_got, core), pivot_other, 1)

    held = grow(got)
    others = []
    for p in range(PARTS):
        others.append(lax.ppermute(held[p], "col", CORE_PERM))
    places = [gray_place(chip, t, order) for order in ORDERS for t in range(8)]
    places = jnp.stack(places + [core]).astype(jnp.int32)
    pair_high, pair_low = pair_terms(places, owner, parent, held, others)

    row_holds = jnp.any(owner_is.reshape(NSUP, 4, -1), axis=2)
    parent_is = parent[None, :] == jnp.arange(NSUP, dtype=jnp.int32)[:, None]
    col_holds = jnp.any(parent_is.reshape(NSUP, WTOT // TILE, -1), axis=2)
    flags = jnp.any(row_holds[:, :, None] & col_holds[:, None, :], axis=0)
    flags = jnp.concatenate([flags.reshape(-1).astype(jnp.int32), col.astype(jnp.int32)[None]])

    total = corrected(flags, near, pair_high, pair_low).reshape(PARTS * 8, -1, wide)
    rows = []
    for i in range(PARTS):
        rows.append(cube_scatter(lambda t, i=i: pick(total, i * 8 + t), chip, ORDERS[i]))
    rows = jnp.concatenate(rows, 1)
    turned = lax.ppermute(rows, BOTH, turn_perm())

    panel = rows.reshape(2, 96, half)
    panel_other = lax.ppermute(pick(panel, 1 - core), "col", CORE_PERM)
    panel = -in_order(core, pick(panel, core), panel_other, 1)

    def cut(vector, start, size):
        return lax.dynamic_slice_in_dim(vector, start, size)

    owner_c = cut(owner, col * 96, 96)
    place = (row % 2) * 4 + row // 2
    owner_r = cut(owner, place * 192, 192)
    owner_out = cut(owner, row * 192, 192)
    parent_c = cut(parent, col * 96, 96)
    own = owner_c[:, None] == owner_r[None, :]
    own_lower = (owner_c[:, None] == owner_out[None, :]) & (parent_c >= 0)[:, None]
    child = parent_c[:, None] == owner_r[None, :]

    level = level_terms(
        flags, high, low, turned, pivot_turned, owner, upper, owner_r, pair_high, pair_low
    )
    level = col_scatter(level, chip, core)
    pair_t = jnp.where(child, level, 0.0)
    padded = jnp.where(
        place % 2 == 0,
        jnp.pad(pair_t, ((0, 0), (0, 192))),
        jnp.pad(pair_t, ((0, 0), (192, 0))),
    )
    mixed = mixed_product(place // 2, pair_high, pair_low, padded)
    done = jnp.where(own | child, level, 0.0).T.reshape(2, 96, 96)
    mixed = direct_scatter(
        mixed.reshape(8, 192, 96), "row", row, lambda q: [(r, r ^ q) for r in range(8)]
    )
    done = lax.ppermute(done, BOTH, back_perm())
    done_other = lax.ppermute(pick(done, 1 - core), "col", CORE_PERM)
    block = in_order(core, pick(done, core), done_other, 1) - jnp.where(own_lower, mixed.T, 0.0)
    return panel, block


def solution(mesh):
    in_specs = (P("col", "row"), P("col", None), P("col", None), P("col", "row"), P(), P(), P())
    out_specs = (P("col", "row"), P("col", "row"))

    return jax.shard_map(shards, mesh=mesh, in_specs=in_specs, out_specs=out_specs, check_vma=False)
```
